32 devices in a mesh: seq: 4 (over z), chan: 8 (over y, x, core).
Axes of the slice: x: 2, y: 2, z: 4, core: 2. Of those that a mesh axis runs over, the one named last changes fastest.
Arguments:
- q_mr: bfloat16 [2048, 8192], P('seq', 'chan'), may hold values from -6 to 6
- k_mr: bfloat16 [2048, 8192], P('seq', 'chan'), may hold values from -6 to 6
- v_mr: bfloat16 [2048, 8192], P('seq', 'chan')
- q_lr: bfloat16 [2048, 8192], P('seq', 'chan'), may hold values from -6 to 6
- k_lr: bfloat16 [2048, 8192], P('seq', 'chan'), may hold values from -6 to 6
- cotangent: bfloat16 [2048, 8192], P('seq', 'chan'), may hold values from -6 to 6
- mr_filter: bfloat16 [128, 512], P(None, 'chan'), may hold values from -0.5 to 0.5
- decay_rates: float32 [16, 512], P(None, 'chan'), as said below
- residues: float32 [16, 512], P(None, 'chan'), may hold values from -1.5 to 1.5
- norm_gain: float32 [8192], P('chan'), may hold values from 0.1 to 1.9
Outputs:
- grad_q_mr: bfloat16 [2048, 8192], P('seq', 'chan')
- grad_k_mr: bfloat16 [2048, 8192], P('seq', 'chan')
- grad_v_mr: bfloat16 [2048, 8192], P('seq', 'chan')
- grad_q_lr: bfloat16 [2048, 8192], P('seq', 'chan')
- grad_k_lr: bfloat16 [2048, 8192], P('seq', 'chan')
- grad_filter: float32 [128, 512], P(None, 'chan')
- grad_residues: float32 [16, 512], P(None, 'chan')
- grad_gain: float32 [8192], P('chan')
The draws below stay inside these ranges and needn't reach their ends.
Inputs may be any that keep to these rules, and one draw needn't show every extreme that they name: `decay_rates`: positive decay rates.
All inputs are finite; a program needn't handle non-finite values.
Results may differ from the reference program's by a relative error of at most 0.02.
Values may be sent and summed in bfloat16 or wider, within the bound.
No kernel may reach another device: no remote copies, remote signals or barrier semaphores. Data moves between devices by JAX's collectives and lax.ppermute only.
A program may use at most 192 MiB of HBM per device.

```python
import jax
import jax.numpy as jnp
from jax import lax

D = 8192
GROUP_WIDTH = 16
GROUPS = 512
MR_TAPS = 128
MODES = 16
SEQ_LEN = 2048


def draw_decay_rates(key, part):
    pick_key, slow_key, fast_key = jax.random.split(jax.random.fold_in(key, 11), 3)
    share = 0.5
    slow_pick = jax.random.uniform(pick_key, (MODES, GROUPS)) < share
    slow = jnp.exp(jax.random.uniform(slow_key, (MODES, GROUPS), minval=jnp.log(0.1 / SEQ_LEN), maxval=jnp.log(2.0 / SEQ_LEN)))
    fast = jnp.exp(jax.random.uniform(fast_key, (MODES, GROUPS), minval=jnp.log(1.0 / 50.0), maxval=jnp.log(1.0 / 30.0)))
    return jnp.where(slow_pick, slow, fast).astype(jnp.float32)


def draw_v_mr(key, part):
    base_key, row_key, col_key = jax.random.split(jax.random.fold_in(key, 23), 3)
    position = jnp.arange(D, dtype=jnp.float32) / D
    base = jax.random.truncated_normal(base_key, -4.0, 4.0, (SEQ_LEN, D))
    row_scale = jnp.exp(jnp.log(10.0) * jax.random.uniform(row_key, (SEQ_LEN,)))
    col_scale = jnp.exp(jnp.log(3.0) * position + jnp.log(10.0) * jax.random.uniform(col_key, (D,)))
    values = base * row_scale[:, None] * col_scale[None, :] / 40.0
    return values.astype(jnp.bfloat16)


def steps_of(own_key, dims, pieces, low, high):
    level = 1.0
    for dim, blocks in pieces:
        draws = jax.random.uniform(jax.random.fold_in(jax.random.fold_in(own_key, 6), dim), (blocks,), jnp.float32, low / len(pieces), high / len(pieces))
        level = level * jnp.repeat(jnp.exp(draws), dims[dim] // blocks).reshape((-1,) + (1,) * (len(dims) - 1 - dim))
    return level


def noise(rng, extent, scale, limit, cuts=(), kind=jnp.bfloat16):
    drawn = jax.random.normal(rng, extent, jnp.float32) * scale
    if len(cuts) > 0:
        drawn = steps_of(rng, extent, cuts, -0.22, 0.18) * drawn
    return jnp.clip(drawn, min=-limit, max=limit).astype(kind)


def setup_inputs(seed: int = 0) -> dict:
    splits = jax.random.split(jax.random.key(seed), 11)
    q_mr = noise(splits[0], (SEQ_LEN, D), 1.0, 6.0, ((0, 4), (1, 8)))
    k_mr = noise(splits[1], (SEQ_LEN, D), 1.0, 6.0, ((0, 4), (1, 8)))
    v_mr = draw_v_mr(jax.random.fold_in(splits[10], 71), 0)
    q_lr = noise(splits[3], (SEQ_LEN, D), 1.0, 6.0, ((0, 4), (1, 8)))
    k_lr = noise(splits[4], (SEQ_LEN, D), 1.0, 6.0, ((0, 4), (1, 8)))
    cotangent = noise(splits[5], (SEQ_LEN, D), 1.0, 6.0, ((0, 4), (1, 8)))
    mr_filter = noise(splits[6], (MR_TAPS, GROUPS), MR_TAPS ** -0.5, 0.5, ((1, 8),))
    decay_rates = draw_decay_rates(jax.random.fold_in(splits[10], 71), 0)
    residues = noise(splits[8], (MODES, GROUPS), 0.25, 1.5, ((1, 8),), jnp.float32)
    norm_gain = jnp.clip(1.0 + 0.18 * jax.random.normal(splits[9], (D,), jnp.float32), 0.1, 1.9)
    return dict(q_mr=q_mr, k_mr=k_mr, v_mr=v_mr, q_lr=q_lr, k_lr=k_lr, cotangent=cotangent, mr_filter=mr_filter, decay_rates=decay_rates, residues=residues, norm_gain=norm_gain)


EPSILON = 1e-05

def expand(params):
    return jnp.repeat(params, GROUP_WIDTH, axis=-1)

def group_sum(values):
    return lax.optimization_barrier(jnp.sum(values.reshape(values.shape[:-1] + (values.shape[-1] // GROUP_WIDTH, GROUP_WIDTH)), axis=-1))

def causal(filter_rows, signal):
    length = 2 * SEQ_LEN
    spectrum = jnp.fft.rfft(filter_rows, length, axis=0) * jnp.fft.rfft(signal, length, axis=0)
    return jnp.fft.irfft(spectrum, length, axis=0)[:SEQ_LEN]

def lagged(gradient, signal):
    length = 2 * SEQ_LEN
    spectrum = jnp.fft.rfft(gradient, length, axis=0) * jnp.conj(jnp.fft.rfft(signal, length, axis=0))
    return jnp.fft.irfft(spectrum, length, axis=0)[:SEQ_LEN]

def medium_rows(taps):
    expanded = expand(taps.astype(jnp.float32))
    return jnp.concatenate([expanded, jnp.zeros((SEQ_LEN - MR_TAPS, expanded.shape[1]), jnp.float32)], axis=0)

def long_rows(decay_rates, scaled):
    offsets = jnp.arange(SEQ_LEN, dtype=jnp.float32)[:, None]
    summed = jnp.zeros((SEQ_LEN, decay_rates.shape[1]), jnp.float32)
    for mode_index in range(MODES):
        summed = summed + scaled[mode_index][None, :] * jnp.exp(-decay_rates[mode_index][None, :] * offsets)
    return expand(summed)

def mode_sums(correlation, decay_rates):
    offsets = jnp.arange(SEQ_LEN, dtype=jnp.float32)[:, None]
    rows_out = []
    for mode_index in range(MODES):
        weights = jnp.exp(-expand(decay_rates[mode_index])[None, :] * offsets)
        rows_out.append(group_sum(lax.optimization_barrier(jnp.sum(weights * correlation, axis=0))))
    return jnp.stack(rows_out)

def reference(q_mr, k_mr, v_mr, q_lr, k_lr, cotangent, mr_filter, decay_rates, residues, norm_gain):
    stretch_cols = min(D, 512)
    block_total = D // stretch_cols
    stretch_groups = stretch_cols // GROUP_WIDTH
    block_ids = jnp.arange(block_total, dtype=jnp.int32)

    def columns_of(values, block_id):
        return lax.dynamic_slice_in_dim(values, (block_id * stretch_cols).astype(jnp.int32), stretch_cols, 1)

    def groups_of(values, block_id):
        return lax.dynamic_slice_in_dim(values, (block_id * stretch_groups).astype(jnp.int32), stretch_groups, 1)

    def rejoin(stacked):
        return jnp.moveaxis(stacked, 0, 1).reshape(stacked.shape[1], -1)
    key_value = (k_mr.astype(jnp.float32) * v_mr.astype(jnp.float32)).astype(jnp.bfloat16)
    conv_mr = rejoin(lax.map(lambda block_id: causal(medium_rows(groups_of(mr_filter, block_id)), columns_of(key_value, block_id).astype(jnp.float32)), block_ids))
    y_mr = q_mr.astype(jnp.float32) * conv_mr
    root_mean = jnp.sqrt(lax.optimization_barrier(jnp.mean(y_mr * y_mr, axis=1, keepdims=True)) + EPSILON)
    normed = y_mr / root_mean
    v_lr = (normed * norm_gain[None, :]).astype(jnp.bfloat16)
    w_lr = (k_lr.astype(jnp.float32) * v_lr.astype(jnp.float32)).astype(jnp.bfloat16)
    mode_scale = jnp.sqrt(-jnp.expm1(-2.0 * decay_rates))
    scaled = residues * mode_scale

    def long_part(block_id):
        filter_rows = long_rows(groups_of(decay_rates, block_id), groups_of(scaled, block_id))
        value_rows = columns_of(w_lr, block_id).astype(jnp.float32)
        conv_lr = causal(filter_rows, value_rows)
        grad_conv = columns_of(cotangent, block_id).astype(jnp.float32) * columns_of(q_lr, block_id).astype(jnp.float32)
        grad_w = lagged(grad_conv, filter_rows)
        mode_grad = mode_sums(lagged(grad_conv, value_rows), groups_of(decay_rates, block_id))
        return (conv_lr, grad_w, mode_grad)
    conv_parts, grad_parts, mode_parts = lax.map(long_part, block_ids)
    conv_lr = rejoin(conv_parts)
    grad_w = rejoin(grad_parts)
    mode_grad = jnp.moveaxis(mode_parts, 0, 1).reshape(MODES, GROUPS)
    grad_out = cotangent.astype(jnp.float32)
    grad_q_lr = (grad_out * conv_lr).astype(jnp.bfloat16)
    grad_k_lr = (grad_w * v_lr.astype(jnp.float32)).astype(jnp.bfloat16)
    grad_v_lr = grad_w * k_lr.astype(jnp.float32)
    grad_gain = lax.optimization_barrier(jnp.sum(grad_v_lr * normed, axis=0)) / jnp.sqrt(float(SEQ_LEN))
    grad_normed = grad_v_lr * norm_gain[None, :]
    inner_sum = lax.optimization_barrier(jnp.mean(grad_normed * normed, axis=1, keepdims=True))
    grad_y_mr = (grad_normed - normed * inner_sum) / root_mean
    grad_q_mr = (grad_y_mr * conv_mr).astype(jnp.bfloat16)
    grad_conv_mr = (grad_y_mr * q_mr.astype(jnp.float32)).astype(jnp.bfloat16)

    def medium_back(block_id):
        gradient = columns_of(grad_conv_mr, block_id).astype(jnp.float32)
        grad_kv = lagged(gradient, medium_rows(groups_of(mr_filter, block_id)))
        tap_grad = group_sum(lagged(gradient, columns_of(key_value, block_id).astype(jnp.float32))[:MR_TAPS])
        return (grad_kv, tap_grad)
    kv_parts, tap_parts = lax.map(medium_back, block_ids)
    grad_kv = rejoin(kv_parts)
    grad_filter = jnp.moveaxis(tap_parts, 0, 1).reshape(MR_TAPS, GROUPS)
    grad_k_mr = (grad_kv * v_mr.astype(jnp.float32)).astype(jnp.bfloat16)
    grad_v_mr = (grad_kv * k_mr.astype(jnp.float32)).astype(jnp.bfloat16)
    norm_terms = jnp.sqrt(float(SEQ_LEN * GROUP_WIDTH))
    return (grad_q_mr, grad_k_mr, grad_v_mr, grad_q_lr, grad_k_lr, grad_filter / norm_terms, mode_grad * mode_scale / norm_terms, grad_gain)
```

```python
import functools

import jax
import jax.numpy as jnp
from jax import lax
from jax.experimental import pallas as pl
from jax.experimental.pallas import tpu as pltpu
from jax.sharding import PartitionSpec as P

EPSILON = 1e-05
LANES = 128
F32 = jnp.float32
BF16 = jnp.bfloat16
HIGHEST = lax.Precision.HIGHEST


def from_behind(value, axis, steps):
    count = lax.axis_size(axis)
    first, last = (max(0, -steps), min(count, count - steps))
    return lax.ppermute(value, axis, [(source, source + steps) for source in range(first, last)])


def from_xor(value, axis, bits):
    count = lax.axis_size(axis)
    return lax.ppermute(value, axis, [(source, source ^ bits) for source in range(count)])


def dot(left, right):
    return jnp.dot(left, right, preferred_element_type=F32)


def dot_last(left, right, precision=None):
    return lax.dot_general(
        left, right, (((1,), (1,)), ((), ())), preferred_element_type=F32, precision=precision
    )


def iota(shape, dim):
    return lax.broadcasted_iota(jnp.int32, shape, dim)


def side_by_side(value, taps):
    blocks = value.shape[0] // taps
    return jnp.concatenate([value[b * taps : (b + 1) * taps] for b in range(blocks)], axis=1)


class Sizes:
    def __init__(self, rows, taps, width, modes, groups):
        self.rows, self.taps, self.width, self.modes, self.groups = rows, taps, width, modes, groups
        self.blocks = rows // taps
        self.tile_groups = LANES // width
        self.span = self.blocks * LANES

    def lane_group(self, lanes):
        return (iota((1, lanes), 1) % LANES) // self.width

    def expand(self, table, tile):
        pick = iota((self.groups, LANES), 0) == tile * self.tile_groups + (
            iota((self.groups, LANES), 1) // self.width
        )
        return jnp.dot(table, pick.astype(F32), preferred_element_type=F32, precision=HIGHEST)

    def tap_rows(self, taps_table, tile):
        pick = iota((self.tile_groups, self.groups), 1) == tile * self.tile_groups + iota(
            (self.tile_groups, self.groups), 0
        )
        return dot_last(pick.astype(F32).astype(BF16), taps_table)

    def column(self, table, group):
        return table[:, group * self.width : group * self.width + 1]

    def choose(self, parts, lanes, per=1):
        owner = self.lane_group(lanes) // per
        chosen = parts[0]
        for index in range(1, len(parts)):
            chosen = jnp.where(owner == index, parts[index], chosen)
        return chosen

    def reverse_index(self):
        return (self.taps - iota((1, self.taps), 1)) % self.taps

    def circulant(self, row):
        spread = jnp.broadcast_to(row, (self.taps, self.taps))
        return pltpu.roll(spread, 0, 1, stride=1, stride_axis=0)

    def lower(self):
        return iota((self.taps, self.taps), 1) <= iota((self.taps, self.taps), 0)

    def upper(self):
        return iota((self.taps, self.taps), 1) >= iota((self.taps, self.taps), 0)

    def pair_masked(self, cat):
        odd = (self.lane_group(cat.shape[1]) % 2).astype(F32)
        even = (1.0 - odd).astype(BF16)
        return jnp.concatenate([cat * even, cat * odd.astype(BF16)], axis=0)

    def paired_apply(self, tables, cat):
        right = self.pair_masked(cat)
        parts = [
            dot(jnp.concatenate([tables[k], tables[k + 1]], axis=1), right)
            for k in range(0, self.tile_groups, 2)
        ]
        return self.choose(parts, cat.shape[1], 2)

    def mode_sums(self, weights, cat):
        stacked = dot(jnp.concatenate(weights, axis=0).astype(BF16), cat)
        parts = [
            stacked[g * self.modes : (g + 1) * self.modes] for g in range(self.tile_groups)
        ]
        return self.choose(parts, cat.shape[1])

    def mode_spread(self, weights, carried):
        left = jnp.concatenate(weights, axis=0).T.astype(BF16)
        owner = self.lane_group(carried.shape[1])
        right = jnp.concatenate(
            [jnp.where(owner == g, carried, 0.0) for g in range(self.tile_groups)], axis=0
        ).astype(BF16)
        return dot(left, right)

    def lag_rows(self, grid):
        total = grid[0:8]
        for q in range(1, self.taps // 8):
            total = total + pltpu.roll(grid[8 * q : 8 * q + 8], self.taps - 8 * q, 1)
        row = iota((8, self.taps), 0)
        for bit in (1, 2, 4):
            total = jnp.where(
                (row // bit) % 2 == 1, pltpu.roll(total, self.taps - bit, 1), total
            )
        return jnp.sum(total, axis=0, keepdims=True)


def back_kernel(sz, cot, q_lr, lam, scaled, gw_part, t_carry, t_total):
    tile = pl.program_id(0)
    rates = sz.expand(lam[...], tile)
    weight = sz.expand(scaled[...], tile)
    grad = (cot[...].astype(F32) * q_lr[...].astype(F32)).astype(BF16)
    cat = side_by_side(grad, sz.taps)
    offset = iota((1, sz.taps), 1).astype(F32)
    powers = [jnp.exp(-sz.column(rates, g) * offset) for g in range(sz.tile_groups)]
    starts = sz.mode_sums(powers, cat)
    decay = jnp.exp(-rates * float(sz.taps))
    carry = jnp.zeros_like(rates)
    for b in reversed(range(sz.blocks)):
        t_carry[b * sz.modes : (b + 1) * sz.modes] = carry
        carry = starts[:, b * LANES : (b + 1) * LANES] + decay * carry
    t_total[...] = carry
    upper = sz.upper()
    tables = []
    for g in range(sz.tile_groups):
        taps_row = jnp.sum(sz.column(weight, g) * powers[g], axis=0, keepdims=True)
        tables.append(jnp.where(upper, sz.circulant(taps_row), 0.0).astype(BF16))
    inside = sz.paired_apply(tables, cat)
    for b in range(sz.blocks):
        gw_part[b * sz.taps : (b + 1) * sz.taps] = inside[:, b * LANES : (b + 1) * LANES]


def medium_kernel(sz, k_mr, v_mr, edge, taps_table, z_out):
    tile = pl.program_id(0)
    kv = (k_mr[...].astype(F32) * v_mr[...].astype(F32)).astype(BF16)
    own = side_by_side(kv, sz.taps)
    before = jnp.concatenate([edge[...], own[:, : sz.span - LANES]], axis=1)
    window = jnp.concatenate([before, own], axis=0)
    natural = sz.tap_rows(taps_table[...], tile)
    flip = iota((sz.taps, sz.taps), 0) == (sz.taps - iota((sz.taps, sz.taps), 1)) % sz.taps
    rows = dot(natural.astype(BF16), flip.astype(F32).astype(BF16))
    lower = sz.lower()
    parts = []
    for g in range(sz.tile_groups):
        ring = sz.circulant(rows[g : g + 1])
        table = jnp.concatenate(
            [jnp.where(lower, 0.0, ring), jnp.where(lower, ring, 0.0)], axis=1
        ).astype(BF16)
        parts.append(dot(table, window))
    z = sz.choose(parts, sz.span)
    for b in range(sz.blocks):
        z_out[b * sz.taps : (b + 1) * sz.taps] = z[:, b * LANES : (b + 1) * LANES]


def sums_kernel(
    sz, gw_part, t_carry, t_in, lam, scaled, z, q_mr, k_lr, gain, gw, t_full, sums, squares, inner
):
    tile = pl.program_id(0)
    rates = sz.expand(lam[...], tile)
    weight = sz.expand(scaled[...], tile)
    arriving = t_in[...]
    carried = []
    for b in range(sz.blocks):
        remaining = float((sz.blocks - 1 - b) * sz.taps)
        block = t_carry[b * sz.modes : (b + 1) * sz.modes] + jnp.exp(-rates * remaining) * arriving
        t_full[b * sz.modes : (b + 1) * sz.modes] = block
        carried.append(block)
    to_next = (sz.taps - iota((1, sz.taps), 1)).astype(F32)
    inward = [
        sz.column(weight, g) * jnp.exp(-sz.column(rates, g) * to_next)
        for g in range(sz.tile_groups)
    ]
    from_state = sz.mode_spread(inward, jnp.concatenate(carried, axis=1))

    @pl.when(tile == 0)
    def _():
        squares[...] = jnp.zeros_like(squares)
        inner[...] = jnp.zeros_like(inner)

    for b in range(sz.blocks):
        at = slice(b * sz.taps, (b + 1) * sz.taps)
        grad_w = gw_part[at] + from_state[:, b * LANES : (b + 1) * LANES]
        gw[at] = grad_w
        y = q_mr[at].astype(F32) * z[at]
        squares[at] += y * y
        inner[at] += (grad_w * k_lr[at].astype(F32)) * gain[...] * y

    @pl.when(tile == pl.num_programs(0) - 1)
    def _():
        for b in range(sz.blocks):
            at = slice(b * sz.taps, (b + 1) * sz.taps)
            sums[b : b + 1] = jnp.sum(squares[at].T, axis=0, keepdims=True)
            sums[sz.blocks + b : sz.blocks + b + 1] = jnp.sum(inner[at].T, axis=0, keepdims=True)


def norm_kernel(
    sz,
    model_width,
    sums,
    z,
    q_mr,
    k_lr,
    gw,
    gain,
    lam,
    t_full,
    w_out,
    gz_out,
    gk_out,
    gq_out,
    gain_out,
    s_carry,
    s_total,
    mode_out,
    inverse,
    mean_inner,
):
    tile = pl.program_id(0)

    @pl.when(tile == 0)
    def _():
        for b in range(sz.blocks):
            at = slice(b * sz.taps, (b + 1) * sz.taps)
            inv = 1.0 / jnp.sqrt(sums[b : b + 1] / model_width + EPSILON)
            mean = sums[sz.blocks + b : sz.blocks + b + 1] * inv / model_width
            inverse[at] = jnp.broadcast_to(inv, (LANES, sz.taps)).T
            mean_inner[at] = jnp.broadcast_to(mean, (LANES, sz.taps)).T

    rates = sz.expand(lam[...], tile)
    scale = gain[...]
    gain_sum = jnp.zeros((1, LANES), F32)
    w_parts = []
    for b in range(sz.blocks):
        at = slice(b * sz.taps, (b + 1) * sz.taps)
        q = q_mr[at].astype(F32)
        k = k_lr[at].astype(F32)
        z_at, gw_at, inv = z[at], gw[at], inverse[at]
        normed = q * z_at * inv
        v_lr = (normed * scale).astype(BF16).astype(F32)
        w = (k * v_lr).astype(BF16)
        w_out[at] = w
        w_parts.append(w)
        gk_out[at] = (gw_at * v_lr).astype(BF16)
        grad_v = gw_at * k
        gain_sum = gain_sum + jnp.sum(grad_v * normed, axis=0, keepdims=True)
        grad_y = (grad_v * scale - normed * mean_inner[at]) * inv
        gq_out[at] = (grad_y * z_at).astype(BF16)
        gz_out[at] = (grad_y * q).astype(BF16)
    gain_out[...] = gain_sum
    cat = jnp.concatenate(w_parts, axis=1)
    to_end = (sz.taps - 1 - iota((1, sz.taps), 1)).astype(F32)
    ends = sz.mode_sums(
        [jnp.exp(-sz.column(rates, g) * to_end) for g in range(sz.tile_groups)], cat
    )
    decay = jnp.exp(-rates * float(sz.taps))
    carry = jnp.zeros_like(rates)
    crossing = jnp.zeros_like(rates)
    for b in range(sz.blocks):
        end = ends[:, b * LANES : (b + 1) * LANES]
        s_carry[b * sz.modes : (b + 1) * sz.modes] = carry
        crossing = crossing + end * t_full[b * sz.modes : (b + 1) * sz.modes]
        carry = end + decay * carry
    s_total[...] = carry
    mode_out[...] = crossing * jnp.exp(-rates)


def cross_kernel(
    sz, w, gz, cot, q_lr, k_mr, v_mr, edge, lam, scaled, crossing, conv_out, lag_out, mode_out
):
    tile = pl.program_id(0)
    rates = sz.expand(lam[...], tile)
    weight = sz.expand(scaled[...], tile)
    lower = sz.lower()
    w_cat = side_by_side(w[...], sz.taps)
    back = sz.reverse_index().astype(F32)
    powers = [jnp.exp(-sz.column(rates, g) * back) for g in range(sz.tile_groups)]
    tables = []
    for g in range(sz.tile_groups):
        taps_row = jnp.sum(sz.column(weight, g) * powers[g], axis=0, keepdims=True)
        tables.append(jnp.where(lower, sz.circulant(taps_row), 0.0).astype(BF16))
    inside = sz.paired_apply(tables, w_cat)
    for b in range(sz.blocks):
        conv_out[b * sz.taps : (b + 1) * sz.taps] = inside[:, b * LANES : (b + 1) * LANES]

    kv = (k_mr[...].astype(F32) * v_mr[...].astype(F32)).astype(BF16)
    own = side_by_side(kv, sz.taps)
    before = jnp.concatenate([edge[...], own[:, : sz.span - LANES]], axis=1)
    window = jnp.concatenate([before, own], axis=0)
    gz_cat = side_by_side(gz[...], sz.taps)
    grad = (cot[...].astype(F32) * q_lr[...].astype(F32)).astype(BF16)
    g_cat = side_by_side(grad, sz.taps)
    owner = sz.lane_group(sz.span)
    lane = iota((sz.modes, LANES), 1)
    lane_owner = sz.lane_group(LANES)
    packed = jnp.zeros((sz.modes, LANES), F32)
    for g in range(sz.tile_groups):
        mask = (owner == g).astype(F32).astype(BF16)
        grid = dot_last(gz_cat * mask, window)
        ring = jnp.where(lower, grid[:, sz.taps :], grid[:, : sz.taps])
        lag_out[g : g + 1] = sz.lag_rows(ring)
        long_grid = dot_last(g_cat * mask, w_cat)
        lags = sz.lag_rows(jnp.where(lower, long_grid, 0.0))
        per_mode = jnp.sum(powers[g] * lags, axis=1, keepdims=True) + jnp.sum(
            jnp.where(lane_owner == g, crossing[...], 0.0), axis=1, keepdims=True
        )
        packed = jnp.where(lane == g, per_mode, packed)
    mode_out[...] = packed.T[: sz.tile_groups]


def out_kernel(
    sz,
    gz,
    after,
    k_mr,
    v_mr,
    taps_table,
    conv_part,
    s_carry,
    s_in,
    lam,
    scaled,
    cot,
    gk_out,
    gv_out,
    gq_out,
):
    tile = pl.program_id(0)
    rates = sz.expand(lam[...], tile)
    weight = sz.expand(scaled[...], tile)
    arriving = s_in[...]
    carried = jnp.concatenate(
        [
            s_carry[b * sz.modes : (b + 1) * sz.modes]
            + jnp.exp(-rates * float(b * sz.taps)) * arriving
            for b in range(sz.blocks)
        ],
        axis=1,
    )
    since = (iota((1, sz.taps), 1) + 1).astype(F32)
    outward = [
        sz.column(weight, g) * jnp.exp(-sz.column(rates, g) * since)
        for g in range(sz.tile_groups)
    ]
    from_state = sz.mode_spread(outward, carried)
    own = side_by_side(gz[...], sz.taps)
    following = jnp.concatenate([own[:, LANES:], after[...]], axis=1)
    window = jnp.concatenate([own, following], axis=0)
    rows = sz.tap_rows(taps_table[...], tile)
    upper = sz.upper()
    parts = []
    for g in range(sz.tile_groups):
        ring = sz.circulant(rows[g : g + 1])
        table = jnp.concatenate(
            [jnp.where(upper, ring, 0.0), jnp.where(upper, 0.0, ring)], axis=1
        ).astype(BF16)
        parts.append(dot(table, window))
    grad_kv = sz.choose(parts, sz.span)
    for b in range(sz.blocks):
        at = slice(b * sz.taps, (b + 1) * sz.taps)
        lanes = slice(b * LANES, (b + 1) * LANES)
        gk_out[at] = (grad_kv[:, lanes] * v_mr[at].astype(F32)).astype(BF16)
        gv_out[at] = (grad_kv[:, lanes] * k_mr[at].astype(F32)).astype(BF16)
        conv = conv_part[at] + from_state[:, lanes]
        gq_out[at] = (cot[at].astype(F32) * conv).astype(BF16)


def params_kernel(sz, lag_scale, gain_scale, count, *refs):
    lag_refs, mode_refs, gain_refs = (refs[k * count : (k + 1) * count] for k in range(3))
    mode_scale, lag_out, mode_out, gain_out = refs[3 * count :]

    def total(parts):
        level = [part[...].astype(F32) for part in parts]
        while len(level) > 1:
            level = [level[k] + level[k + 1] for k in range(0, len(level), 2)]
        return level[0]

    flip = iota((sz.taps, sz.taps), 1) == (sz.taps - iota((sz.taps, sz.taps), 0)) % sz.taps
    lag_out[...] = dot_last(flip.astype(F32), total(lag_refs), HIGHEST) * lag_scale
    mode_out[...] = total(mode_refs).T * mode_scale[...] * lag_scale
    gain_out[...] = total(gain_refs) * gain_scale


def shards(q_mr, k_mr, v_mr, q_lr, k_lr, cotangent, mr_filter, decay_rates, residues, norm_gain):
    row_count, chan_count = q_mr.shape
    taps_len, group_count = mr_filter.shape
    modes = decay_rates.shape[0]
    seq_count = lax.axis_size("seq")
    chan_parts = lax.axis_size("chan")
    model_width = chan_count * chan_parts
    sz = Sizes(row_count, taps_len, chan_count // group_count, modes, group_count)
    tiles = chan_count // LANES
    states = sz.blocks * modes

    def tile_of(rows):
        return pl.BlockSpec((rows, LANES), lambda i: (0, i))

    def whole(shape):
        return pl.BlockSpec(shape, lambda i: (0,) * len(shape))

    def struct(rows, dtype):
        return jax.ShapeDtypeStruct((rows, chan_count), dtype)

    big, edge_spec, state_spec, carry_spec = (
        tile_of(row_count),
        tile_of(taps_len),
        tile_of(modes),
        tile_of(states),
    )
    row_spec = tile_of(1)
    rate_spec, tap_spec = whole((modes, group_count)), whole((taps_len, group_count))
    sum_spec = whole((2 * sz.blocks, taps_len))

    def call(kernel, in_specs, out_specs, out_shape, scratch=(), flops=0, moved=0):
        return pl.pallas_call(
            kernel,
            grid=(tiles,),
            in_specs=in_specs,
            out_specs=out_specs,
            out_shape=out_shape,
            scratch_shapes=list(scratch),
            cost_estimate=pl.CostEstimate(
                flops=flops, bytes_accessed=moved, transcendentals=0
            ),
        )

    unit = row_count * chan_count
    mode_scale = jnp.sqrt(-jnp.expm1(-2.0 * decay_rates))
    scaled = residues * mode_scale
    gain_row = norm_gain.reshape(1, chan_count)
    tail = slice(row_count - taps_len, row_count)
    edge = from_behind(
        (k_mr[tail].astype(F32) * v_mr[tail].astype(F32)).astype(BF16), "seq", 1
    )

    gw_part, t_carry, t_total = call(
        functools.partial(back_kernel, sz),
        [big, big, rate_spec, rate_spec],
        [big, carry_spec, state_spec],
        [struct(row_count, F32), struct(states, F32), struct(modes, F32)],
        flops=unit * 2000,
        moved=unit * 8,
    )(cotangent, q_lr, decay_rates, scaled)

    hop = jnp.repeat(jnp.exp(-decay_rates * float(row_count)), sz.width, axis=1)

    def arriving(total, direction):
        incoming = jnp.zeros_like(total)
        for steps in range(seq_count - 1, 0, -1):
            incoming = incoming * hop + from_behind(total, "seq", direction * steps)
        return incoming

    t_in = arriving(t_total, -1)

    z = call(
        functools.partial(medium_kernel, sz),
        [big, big, edge_spec, tap_spec],
        big,
        struct(row_count, F32),
        flops=unit * 4000,
        moved=unit * 8,
    )(k_mr, v_mr, edge, mr_filter)

    gw, t_full, sums = call(
        functools.partial(sums_kernel, sz),
        [big, carry_spec, state_spec, rate_spec, rate_spec, big, big, big, row_spec],
        [big, carry_spec, sum_spec],
        [
            struct(row_count, F32),
            struct(states, F32),
            jax.ShapeDtypeStruct((2 * sz.blocks, taps_len), F32),
        ],
        [pltpu.VMEM((row_count, LANES), F32)] * 2,
        flops=unit * 300,
        moved=unit * 16,
    )(gw_part, t_carry, t_in, decay_rates, scaled, z, q_mr, k_lr, gain_row)

    bits = 1
    while bits < chan_parts:
        sums = sums + from_xor(sums, "chan", bits)
        bits *= 2

    w, gz, grad_k_lr, grad_q_mr, gain_part, s_carry, s_total, crossing = call(
        functools.partial(norm_kernel, sz, float(model_width)),
        [sum_spec, big, big, big, big, row_spec, rate_spec, carry_spec],
        [big, big, big, big, row_spec, carry_spec, state_spec, state_spec],
        [
            struct(row_count, BF16),
            struct(row_count, BF16),
            struct(row_count, BF16),
            struct(row_count, BF16),
            struct(1, F32),
            struct(states, F32),
            struct(modes, F32),
            struct(modes, F32),
        ],
        [pltpu.VMEM((row_count, LANES), F32)] * 2,
        flops=unit * 300,
        moved=unit * 20,
    )(sums, z, q_mr, k_lr, gw, gain_row, decay_rates, t_full)

    after = from_behind(gz[:taps_len], "seq", -1)
    s_in = arriving(s_total, 1)

    conv_part, lags, mode_part = call(
        functools.partial(cross_kernel, sz),
        [big] * 6 + [edge_spec, rate_spec, rate_spec, state_spec],
        [
            big,
            pl.BlockSpec((sz.tile_groups, taps_len), lambda i: (i, 0)),
            pl.BlockSpec((sz.tile_groups, modes), lambda i: (i, 0)),
        ],
        [
            struct(row_count, F32),
            jax.ShapeDtypeStruct((group_count, taps_len), F32),
            jax.ShapeDtypeStruct((group_count, modes), F32),
        ],
        flops=unit * 8000,
        moved=unit * 16,
    )(w, gz, cotangent, q_lr, k_mr, v_mr, edge, decay_rates, scaled, crossing)

    parts = [
        lags.astype(BF16),
        mode_part.astype(BF16),
        gain_part.reshape(tiles, LANES).astype(BF16),
    ]
    gathered = []
    for part in parts:
        gathered += [part] + [from_xor(part, "seq", bits) for bits in range(1, seq_count)]

    grad_k_mr, grad_v_mr, grad_q_lr = call(
        functools.partial(out_kernel, sz),
        [
            big,
            edge_spec,
            big,
            big,
            tap_spec,
            big,
            carry_spec,
            state_spec,
            rate_spec,
            rate_spec,
            big,
        ],
        [big] * 3,
        [struct(row_count, BF16)] * 3,
        flops=unit * 4000,
        moved=unit * 18,
    )(gz, after, k_mr, v_mr, mr_filter, conv_part, s_carry, s_in, decay_rates, scaled, cotangent)

    total_rows = float(row_count * seq_count)
    grad_filter, grad_residues, grad_gain = pl.pallas_call(
        functools.partial(
            params_kernel,
            sz,
            (total_rows * sz.width) ** -0.5,
            total_rows**-0.5,
            seq_count,
        ),
        out_shape=[
            jax.ShapeDtypeStruct((taps_len, group_count), F32),
            jax.ShapeDtypeStruct((modes, group_count), F32),
            jax.ShapeDtypeStruct((tiles, LANES), F32),
        ],
    )(*gathered, mode_scale)
    return (
        grad_q_mr,
        grad_k_mr,
        grad_v_mr,
        grad_q_lr,
        grad_k_lr,
        grad_filter,
        grad_residues,
        grad_gain.reshape(chan_count),
    )


def solution(mesh):
    blocks = (P("seq", "chan"),) * 6
    return jax.shard_map(
        shards,
        mesh=mesh,
        in_specs=blocks + (P(None, "chan"),) * 3 + (P("chan"),),
        out_specs=blocks[:5] + (P(None, "chan"),) * 2 + (P("chan"),),
        check_vma=False,
    )
```
